32 devices in a mesh: gx: 8 (over z, x), gy: 4 (over y, core).
Axes of the slice: x: 2, y: 2, z: 4, core: 2. Of those that a mesh axis runs over, the one named last changes fastest.
Arguments:
- velocity: float32 [3, 128, 128, 256], P(None, 'gx', 'gy'), may hold values from -6 to 6
- owner_block: int32 [65536, 1], P(('gx', 'gy')), may hold values from 0 to 31, as said below
- base_x: int32 [65536], P(('gx', 'gy')), may hold values from 0 to 16
- base_y: int32 [65536], P(('gx', 'gy')), may hold values from 0 to 32
- base_z: int32 [65536], P(('gx', 'gy')), may hold values from 0 to 255
- delta_weights: float32 [12, 65536], P(None, ('gx', 'gy')), may hold values from 0.1 to 1
- marker_offset: float32 [3, 65536], P(None, ('gx', 'gy')), may hold values from -4 to 4
- sphere_motion: float32 [6, 64], P(None, ('gx', 'gy')), may hold values from -6 to 6
- contact_sphere: int32 [128], P(('gx', 'gy')), may hold values from 0 to 63, as said below
- contact_partner: int32 [128], P(('gx', 'gy')), may hold values from 0 to 63
Outputs:
- velocity_star: float32 [3, 128, 128, 256], P(None, 'gx', 'gy')
- new_motion: float32 [6, 64], P(None, ('gx', 'gy'))
The draws below stay inside these ranges and needn't reach their ends.
Inputs may be any that keep to these rules, and one draw needn't show every extreme that they name: `owner_block`: block b stands at gx index b // 4 and gy index b % 4. Each marker's owner block is the block of the device that holds the marker or one of the eight blocks beside it (periodic along gx, none beyond the walls along gy). Among the markers of one device, at most 256 have any one owner block other than that device's own, and in every device exactly 256 have one such block. `contact_sphere`: entry k names one of the 2 spheres k // 4 * 2 and after, those of the device that holds entry k.
All inputs are finite; a program needn't handle non-finite values.
Results may differ from the reference program's by a relative error of at most 0.0003.
Values sent between devices are 32-bit elements; how exact they have to be, the bound alone decides.
A program may use at most 64 MiB of HBM per device.

```python
import math
import jax
import jax.numpy as jnp
from jax import lax

CX = 16
CY = 32
NZ = 256
MK = 1024
S_DEV = 2
CT_DEV = 4
ITERS = 4
NX = 128
NY = 128
SPHERES = 64
MARKERS = 65536
CAP = 256
CONTACTS = 128
N_GX = 8
N_GY = 4


def draw_contact_sphere(key, part):
    entries = jnp.arange(CONTACTS, dtype=jnp.int32)
    picked = jax.random.randint(key, (CONTACTS,), 0, S_DEV, dtype=jnp.int32)
    return entries // CT_DEV * S_DEV + picked


def draw_owner_block(key, part):
    per_device = S_DEV * MK
    devices = N_GX * N_GY
    device = jnp.arange(devices, dtype=jnp.int32)
    column = device // N_GY
    row = device % N_GY
    shift_x = jnp.array([-1, -1, -1, 0, 0, 1, 1, 1], dtype=jnp.int32)
    shift_y = jnp.array([-1, 0, 1, -1, 1, -1, 0, 1], dtype=jnp.int32)
    counts = jax.random.randint(jax.random.fold_in(key, 11), (devices, 8), 1, CAP + 1, dtype=jnp.int32)
    coin = jax.random.randint(jax.random.fold_in(key, 12), (devices,), 0, 2, dtype=jnp.int32)
    full_lane = jnp.where(coin == 0, 1, 6).astype(jnp.int32)
    counts = jnp.where(jnp.arange(8, dtype=jnp.int32)[None, :] == full_lane[:, None], CAP, counts)
    device_keys = jax.random.split(jax.random.fold_in(key, 13), devices)
    position = jax.vmap(lambda one_key: jax.random.permutation(one_key, per_device))(device_keys).astype(jnp.int32)
    lane = jnp.minimum(position // CAP, 7)
    within = position % CAP
    count_here = jnp.take_along_axis(counts, lane, axis=1)
    away = within < count_here
    towards_x = (column[:, None] + shift_x[lane]) % N_GX
    towards_y = row[:, None] + shift_y[lane]
    inside = jnp.logical_and(towards_y >= 0, towards_y < N_GY)
    chosen = jnp.where(jnp.logical_and(away, inside), towards_x * N_GY + towards_y, device[:, None])
    return chosen.reshape(MARKERS, 1).astype(jnp.int32)


def plant(values, stream_key, low, largest):
    shape = values.shape
    index_at = [jax.random.randint(jax.random.fold_in(stream_key, axis), (), 0, shape[axis]) for axis in range(len(shape))]
    values = values.at[tuple(index_at)].set(low)
    longest = shape.index(max(shape))
    index_at[longest] = (index_at[longest] + 1) % shape[longest]
    return values.at[tuple(index_at)].set(largest)


def block_levels(key, extent, shards, smallest, high):
    gain = 1.0
    for axis_at, shards_of in shards:
        heights = jax.random.uniform(jax.random.fold_in(jax.random.fold_in(key, 6), axis_at), (shards_of,), jnp.float32, smallest / len(shards), high / len(shards))
        gain = gain * jnp.repeat(jnp.exp(heights), extent[axis_at] // shards_of).reshape((-1,) + (1,) * (len(extent) - 1 - axis_at))
    return gain


def noise(rng, dims, scale, limit, cuts=(), held_as=jnp.bfloat16):
    level = block_levels(rng, dims, cuts, -0.22, 0.18) if cuts else 1.0
    result = jax.random.normal(rng, dims, jnp.float32) * scale * level
    return jnp.minimum(jnp.maximum(result, -limit), limit).astype(held_as)


def setup_inputs(seed: int = 0) -> dict:
    seeds = jax.random.split(jax.random.key(seed), 11)
    return {
        "velocity": noise(seeds[0], (3, NX, NY, NZ), 1.0, 6.0, ((1, 8), (2, 4)), jnp.float32),
        "owner_block": draw_owner_block(jax.random.fold_in(seeds[10], 71), 0),
        "base_x": plant(jax.random.randint(seeds[2], (MARKERS,), 0, CX + 1), jax.random.fold_in(seeds[2], 1), 0, CX).astype(jnp.int32),
        "base_y": plant(jax.random.randint(seeds[3], (MARKERS,), 0, CY + 1), jax.random.fold_in(seeds[3], 1), 0, CY).astype(jnp.int32),
        "base_z": plant(jax.random.randint(seeds[4], (MARKERS,), 0, NZ), jax.random.fold_in(seeds[4], 1), 0, NZ - 1).astype(jnp.int32),
        "delta_weights": jnp.clip(jnp.exp(math.log(1.0) - 2.3025851 * jax.random.uniform(seeds[5], (12, MARKERS), jnp.float32) ** block_levels(seeds[5], (12, MARKERS), ((1, 32),), -0.2, 0.2)), 0.1, 1.0),
        "marker_offset": noise(seeds[6], (3, MARKERS), 1.0, 4.0, ((1, 32),), jnp.float32),
        "sphere_motion": noise(seeds[7], (6, SPHERES), 1.0, 6.0, ((1, 32),), jnp.float32),
        "contact_sphere": draw_contact_sphere(jax.random.fold_in(seeds[10], 71), 0),
        "contact_partner": plant(jax.random.randint(seeds[9], (CONTACTS,), 0, SPHERES), jax.random.fold_in(seeds[9], 1), 0, SPHERES - 1).astype(jnp.int32),
    }


DIFFUSION = 1.0
RESPONSE = 0.5
DASHPOT = 0.1


def support(start_x, start_y, start_z, weights, stride_y, extent_z):
    offsets = jnp.arange(4, dtype=jnp.int32)
    cells_x = start_x[None, :] + offsets[:, None]
    cells_y = start_y[None, :] + offsets[:, None]
    cells_z = (start_z[None, :] + offsets[:, None]) % extent_z
    where = ((cells_x[:, None, None, :] * stride_y + cells_y[None, :, None, :]) * extent_z + cells_z[None, None, :, :]).reshape(64, -1)
    product = (weights[0:4][:, None, None, :] * weights[4:8][None, :, None, :] * weights[8:12][None, None, :, :]).reshape(64, -1)
    return where, product


def reference(velocity, owner_block, base_x, base_y, base_z, delta_weights, marker_offset, sphere_motion, contact_sphere, contact_partner):
    padded = jnp.pad(velocity, ((0, 0), (2, 2), (0, 0), (0, 0)), mode="wrap")
    padded = jnp.pad(padded, ((0, 0), (0, 0), (2, 2), (0, 0)))
    flat_field = padded.reshape(3, -1)
    owner = owner_block[:, 0]
    start_x = (owner // N_GY) * CX + base_x
    start_y = (owner % N_GY) * CY + base_y
    linear = sphere_motion[0:3]
    angular = sphere_motion[3:6]
    marker_linear = jnp.repeat(linear, MK, axis=1)
    marker_angular = jnp.repeat(angular, MK, axis=1)
    target = marker_linear + jnp.cross(marker_angular, marker_offset, axis=0)
    block_x = start_x.reshape(SPHERES, MK)
    block_y = start_y.reshape(SPHERES, MK)
    block_z = base_z.reshape(SPHERES, MK)
    block_w = delta_weights.reshape(12, SPHERES, MK).transpose(1, 0, 2)
    block_t = target.reshape(3, SPHERES, MK).transpose(1, 0, 2)

    def sample(item):
        where, product = support(item[0], item[1], item[2], item[3], NY + 4, NZ)
        picked = flat_field[:, where]
        return jnp.sum(picked * product[None], axis=1)

    sampled = lax.map(sample, (block_x, block_y, block_z, block_w))
    block_force = block_t - sampled
    force = block_force.transpose(1, 0, 2).reshape(3, MARKERS)
    push = jnp.sum(block_force, axis=-1).T / MK
    twist = jnp.sum(jnp.cross(marker_offset, force, axis=0).reshape(3, SPHERES, MK), axis=-1) / MK
    moved = linear - RESPONSE * push
    turned = angular - RESPONSE * twist
    spring = moved[:, contact_partner] - moved[:, contact_sphere]
    settled = moved + DASHPOT * jax.ops.segment_sum(spring.T, contact_sphere, SPHERES).T
    new_motion = jnp.concatenate([settled, turned], axis=0)

    def deposit(field, item):
        where, product = support(item[0], item[1], item[2], item[3], NY + 4, NZ)
        return field.at[:, where.reshape(-1)].add((product[None] * item[4][:, None, :]).reshape(3, -1)), None

    spread, unused = lax.scan(deposit, jnp.zeros_like(flat_field), (block_x, block_y, block_z, block_w, block_force))
    spread = spread.reshape(padded.shape)
    folded = spread[:, 2:NX + 2]
    folded = folded.at[:, 0:2].add(spread[:, NX + 2:NX + 4])
    folded = folded.at[:, NX - 2:NX].add(spread[:, 0:2])
    source = folded[:, :, 2:NY + 2]
    rhs = velocity + source
    state = rhs
    for sweep in range(ITERS):
        walled = jnp.pad(state, ((0, 0), (0, 0), (1, 1), (0, 0)))
        beside_all = jnp.roll(state, -1, 1) + jnp.roll(state, 1, 1) + walled[:, :, 2:] + walled[:, :, :-2]
        beside_all = beside_all + jnp.roll(state, -1, 3) + jnp.roll(state, 1, 3)
        state = (rhs + DIFFUSION * beside_all) / (1.0 + 6.0 * DIFFUSION)
    return state, new_motion
```

```python
import functools

import jax
import jax.numpy as jnp
import numpy as np
from jax import lax
from jax.experimental import pallas as pl
from jax.experimental.pallas import tpu as pltpu
from jax.sharding import PartitionSpec as P

ITERS = 4


DIFFUSION = 1.0
RESPONSE = 0.5
DASHPOT = 0.1
TILE_ROWS = 16
TILE_LANES = 128


def shift(array, axis, step, periodic):
    size = lax.axis_size(axis)
    pairs = [(i, (i + step) % size) for i in range(size) if periodic or 0 <= i + step < size]
    return lax.ppermute(array, axis, pairs)


def with_halo(array, axis, dim, width, periodic):
    length = array.shape[dim]
    last = lax.slice_in_dim(array, length - width, length, axis=dim)
    leading = lax.slice_in_dim(array, 0, width, axis=dim)
    before = shift(last, axis, 1, periodic)
    after = shift(leading, axis, -1, periodic)
    return jnp.concatenate([before, array, after], axis=dim)


def weight_table(start, weights, extent, wrapped):
    positions = jnp.arange(extent, dtype=jnp.int32)[:, None]
    table = jnp.zeros((extent, start.shape[0]), jnp.float32)
    for offset in range(4):
        target_cell = start + offset
        if wrapped:
            target_cell = target_cell % extent
        table = table + weights[offset][None, :] * (positions == target_cell[None, :]).astype(
            jnp.float32
        )
    return table


def tables(start_x, start_y, start_z, weights, span_x, span_y, extent_z):
    return (
        weight_table(start_x, weights[0:4], span_x + 4, False),
        weight_table(start_y, weights[4:8], span_y + 4, False),
        weight_table(start_z, weights[8:12], extent_z, True),
    )


def sample_field(field, table_x, table_y, table_z):
    extent_z = field.shape[3]
    partial_z = jnp.dot(field.reshape(-1, extent_z), table_z, precision=lax.Precision.HIGH)
    partial_z = partial_z.reshape(3, field.shape[1], field.shape[2], -1)
    partial_y = jnp.sum(partial_z * table_y[None, None, :, :], axis=2)
    return jnp.sum(partial_y * table_x[None, :, :], axis=1)


def deposit_field(forces, table_x, table_y, table_z):
    spread_xy = forces[:, None, None, :] * table_x[None, :, None, :] * table_y[None, None, :, :]
    count = forces.shape[1]
    flat = lax.dot_general(
        spread_xy.reshape(-1, count),
        table_z,
        (((1,), (1,)), ((), ())),
        precision=lax.Precision.HIGH,
    )
    return flat.reshape(3, table_x.shape[0], table_y.shape[0], table_z.shape[0])


def relax_kernel(e_ref, below_ref, above_ref, mask_ref, out_ref, rhs, one, two):
    span_x, span_y = out_ref.shape[1], out_ref.shape[2]
    wide_x, wide_y = span_x + 2 * ITERS, span_y + 2 * ITERS
    rim = below_ref.shape[2]
    mask = mask_ref[...]
    extent_z = mask.shape[1]

    def build(x, carry):
        one[x] = jnp.zeros((wide_y, extent_z), jnp.float32)
        one[x, 2 : wide_y - 2] = e_ref[0, x]
        one[x, 0:rim] = one[x, 0:rim] + below_ref[0, x]
        one[x, wide_y - rim : wide_y] = one[x, wide_y - rim : wide_y] + above_ref[0, x]
        rhs[x] = one[x] * mask
        return carry

    lax.fori_loop(0, wide_x, build, 0)
    inverse = 1.0 / (1.0 + 6.0 * DIFFUSION)

    def row(source, x):
        here = source[x]
        beside = source[x - 1] + source[x + 1]
        beside = beside + pltpu.roll(here, 1, 0) + pltpu.roll(here, wide_y - 1, 0)
        beside = beside + pltpu.roll(here, 1, 1) + pltpu.roll(here, extent_z - 1, 1)
        return (rhs[x] + DIFFUSION * beside) * (inverse * mask)

    source = rhs
    for sweep in range(ITERS - 1):
        target = one if sweep % 2 == 0 else two

        def step(pair, carry, source=source, target=target, first=sweep + 1):
            x = first + 2 * pair
            new = (row(source, x), row(source, x + 1))
            target[x] = new[0]
            target[x + 1] = new[1]
            return carry

        lax.fori_loop(0, wide_x // 2 - sweep - 1, step, 0)
        source = target

    def last(pair, carry, source=source):
        x = 2 * pair
        new = (row(source, x + ITERS), row(source, x + ITERS + 1))
        out_ref[0, x] = new[0][ITERS : ITERS + span_y]
        out_ref[0, x + 1] = new[1][ITERS : ITERS + span_y]
        return carry

    lax.fori_loop(0, span_x // 2, last, 0)


def relax_all(grown, below, above, mask, span_x, span_y):
    extent_z = grown.shape[3]
    wide = (span_x + 2 * ITERS, span_y + 2 * ITERS, extent_z)

    def block(array):
        return pl.BlockSpec((1,) + array.shape[1:], lambda c: (c, 0, 0, 0))

    return pl.pallas_call(
        relax_kernel,
        grid=(grown.shape[0],),
        out_shape=jax.ShapeDtypeStruct((grown.shape[0], span_x, span_y, extent_z), jnp.float32),
        in_specs=[
            block(grown),
            block(below),
            block(above),
            pl.BlockSpec(mask.shape, lambda c: (0, 0)),
        ],
        out_specs=pl.BlockSpec((1, span_x, span_y, extent_z), lambda c: (c, 0, 0, 0)),
        scratch_shapes=[pltpu.VMEM(wide, jnp.float32)] * 3,
        cost_estimate=pl.CostEstimate(
            flops=40 * grown.size, bytes_accessed=12 * grown.size, transcendentals=0
        ),
        name="relax",
    )(grown, below, above, mask)


def gather_kernel(columns, rows, x_ref, out_ref, held, local_sem, row_send, row_recv, col_send, col_recv):
    column = lax.axis_index("gx")
    row = lax.axis_index("gy")
    row_peers = [lax.rem(row + k, rows) for k in range(1, rows)]
    column_peers = [lax.rem(column + k, columns) for k in range(1, columns)]
    barrier = pltpu.get_barrier_semaphore()
    mesh = pl.DeviceIdType.MESH
    for peer in row_peers:
        pl.semaphore_signal(barrier, inc=1, device_id=(column, peer), device_id_type=mesh)
    for peer in column_peers:
        pl.semaphore_signal(barrier, inc=1, device_id=(peer, row), device_id_type=mesh)
    own = pltpu.make_async_copy(x_ref, held.at[column, row], local_sem)
    own.start()
    pl.semaphore_wait(barrier, rows + columns - 2)
    first = []
    for k, peer in enumerate(row_peers):
        copy = pltpu.make_async_remote_copy(
            src_ref=x_ref,
            dst_ref=held.at[column, row],
            send_sem=row_send.at[k],
            recv_sem=row_recv.at[k],
            device_id=(column, peer),
            device_id_type=mesh,
        )
        copy.start()
        first.append(copy)
    own.wait()
    for copy in first:
        copy.wait()
    second = []
    for k, peer in enumerate(column_peers):
        copy = pltpu.make_async_remote_copy(
            src_ref=held.at[column],
            dst_ref=held.at[column],
            send_sem=col_send.at[k],
            recv_sem=col_recv.at[k],
            device_id=(peer, row),
            device_id_type=mesh,
        )
        copy.start()
        second.append(copy)
    for copy in second:
        copy.wait()
    out_ref[...] = held[...]


def gather_tiles(tile):
    columns, rows = lax.axis_size("gx"), lax.axis_size("gy")
    shape = (columns, rows) + tile.shape
    return pl.pallas_call(
        functools.partial(gather_kernel, columns, rows),
        out_shape=jax.ShapeDtypeStruct(shape, jnp.float32),
        in_specs=[pl.BlockSpec(memory_space=pltpu.VMEM)],
        out_specs=pl.BlockSpec(memory_space=pltpu.VMEM),
        scratch_shapes=[
            pltpu.VMEM(shape, jnp.float32),
            pltpu.SemaphoreType.DMA,
            pltpu.SemaphoreType.DMA((rows - 1,)),
            pltpu.SemaphoreType.DMA((rows - 1,)),
            pltpu.SemaphoreType.DMA((columns - 1,)),
            pltpu.SemaphoreType.DMA((columns - 1,)),
        ],
        compiler_params=pltpu.CompilerParams(collective_id=0, has_side_effects=True),
        cost_estimate=pl.CostEstimate(flops=0, bytes_accessed=40_000_000, transcendentals=0),
        name="gather_tiles",
    )(tile)


ARRIVALS = ((0, 0), (1, 0), (2, 0), (0, 1), (2, 1), (0, 2), (1, 2), (2, 2), (1, 1))


def combine_matrix(columns, rows, per_sphere):
    matrix = np.zeros((columns, rows, columns, rows, TILE_ROWS), np.float32)
    for i in range(columns):
        for j in range(rows):
            for slot, (a, b) in enumerate(ARRIVALS):
                target_row = j + b - 1
                if 0 <= target_row < rows:
                    matrix[(i + a - 1) % columns, target_row, i, j, slot] -= RESPONSE / per_sphere
            matrix[i, j, i, j, len(ARRIVALS)] = 1.0
    return matrix.reshape(columns * rows, -1)


def moments(forces, offsets):
    return jnp.concatenate([forces, jnp.cross(offsets, forces, axis=0)], axis=0)


def on_device(
    velocity,
    owner_block,
    base_x,
    base_y,
    base_z,
    delta_weights,
    marker_offset,
    sphere_motion,
    contact_sphere,
    contact_partner,
):
    span_x = velocity.shape[1]
    span_y = velocity.shape[2]
    extent_z = velocity.shape[3]
    row_count = lax.axis_size("gy")
    column_count = lax.axis_size("gx")
    here = lax.axis_index(("gx", "gy"))
    row_index = lax.axis_index("gy")
    column_index = lax.axis_index("gx")
    grown_field = with_halo(velocity, "gx", 1, 2, True)
    grown_field = with_halo(grown_field, "gy", 2, 2, False)
    markers = base_x.shape[0]
    spheres_here = sphere_motion.shape[1]
    per_sphere = markers // spheres_here
    capacity = markers // 8
    owner = owner_block[:, 0]
    at_home = owner == here
    home_weight = at_home.astype(jnp.float32)
    lanes = 8
    step_x = (owner // row_count - column_index + 1 + column_count) % column_count
    step_y = owner % row_count - row_index + 1
    lane = step_x * 3 + step_y
    lane = lane - (lane > 4).astype(jnp.int32)
    hits = (lane[:, None] == jnp.arange(lanes, dtype=jnp.int32)[None, :]).astype(jnp.int32)
    hits = hits * (1 - at_home.astype(jnp.int32))[:, None]
    ranked = jnp.sum((jnp.cumsum(hits, axis=0) - hits) * hits, axis=1)
    total_slots = lanes * capacity
    slots = jnp.where(at_home, total_slots, lane * capacity + ranked)
    marker_motion = jnp.broadcast_to(
        sphere_motion[:, :, None], (6, spheres_here, per_sphere)
    ).reshape(6, markers)
    target = marker_motion[0:3] + jnp.cross(marker_motion[3:6], marker_offset, axis=0)
    coords = jnp.stack([base_x, base_y, base_z]).astype(jnp.float32)
    sphere_of = (jnp.arange(markers, dtype=jnp.int32) // per_sphere).astype(jnp.float32)
    payload = jnp.concatenate(
        [delta_weights, coords, target, marker_offset, sphere_of[None, :]], axis=0
    )
    outgoing = (
        jnp.zeros((payload.shape[0], total_slots), jnp.float32)
        .at[:, slots]
        .set(payload, mode="drop")
    )
    c = capacity
    from_left = shift(outgoing[:, 5 * c :], "gx", 1, True)
    from_right = shift(outgoing[:, : 3 * c], "gx", -1, True)
    down = [from_left[:, :c], outgoing[:, 3 * c : 4 * c], from_right[:, :c]]
    up = [from_left[:, 2 * c :], outgoing[:, 4 * c : 5 * c], from_right[:, 2 * c :]]
    from_above = shift(jnp.concatenate(down, axis=1), "gy", -1, False)
    from_below = shift(jnp.concatenate(up, axis=1), "gy", 1, False)
    arrived = jnp.concatenate(
        [from_below, from_left[:, c : 2 * c], from_right[:, c : 2 * c], from_above], axis=1
    )

    home_tables = tables(base_x, base_y, base_z, delta_weights, span_x, span_y, extent_z)
    sampled_home = sample_field(grown_field, *home_tables)
    home_force = (target - sampled_home) * home_weight[None, :]
    cell_start = arrived[12:15].astype(jnp.int32)
    slot_tables = tables(
        cell_start[0], cell_start[1], cell_start[2], arrived[0:12], span_x, span_y, extent_z
    )
    slot_force = arrived[15:18] - sample_field(grown_field, *slot_tables)
    forces_all = jnp.concatenate([home_force, slot_force], axis=1)
    all_tables = [jnp.concatenate(pair, axis=1) for pair in zip(home_tables, slot_tables)]
    spread = deposit_field(forces_all, *all_tables)

    spread = spread + jnp.pad(velocity, ((0, 0), (2, 2), (2, 2), (0, 0)))
    reach = ITERS + 2
    left = shift(spread[:, span_x + 4 - reach :], "gx", 1, True)
    right = shift(spread[:, :reach], "gx", -1, True)
    grown = jnp.concatenate(
        [
            left[:, :2],
            spread[:, : reach - 2] + left[:, 2:],
            spread[:, reach - 2 : span_x + 6 - reach],
            spread[:, span_x + 6 - reach :] + right[:, : reach - 2],
            right[:, reach - 2 :],
        ],
        axis=1,
    )
    below = shift(grown[:, :, span_y + 4 - reach :], "gy", 1, False)
    above = shift(grown[:, :, :reach], "gy", -1, False)
    global_row = row_index * span_y - ITERS + jnp.arange(span_y + 2 * ITERS, dtype=jnp.int32)
    inside = jnp.logical_and(global_row >= 0, global_row < span_y * row_count)
    mask = jnp.broadcast_to(inside.astype(jnp.float32)[:, None], (span_y + 2 * ITERS, extent_z))
    state = relax_all(grown, below, above, mask, span_x, span_y)

    home_sums = jnp.sum(
        moments(home_force, marker_offset).reshape(6, spheres_here, per_sphere), axis=-1
    )
    slot_moments = moments(slot_force, arrived[18:21])
    chosen = arrived[21][None, :] == jnp.arange(spheres_here, dtype=jnp.float32)[:, None]
    picked = jnp.where(chosen[None], slot_moments[:, None], 0.0)
    slot_sums = jnp.sum(picked.reshape(6, spheres_here, lanes, capacity), axis=-1)
    columns = jnp.concatenate(
        [slot_sums, home_sums[:, :, None], sphere_motion[:, :, None]], axis=2
    )
    tile = columns.transpose(2, 1, 0).reshape(lanes + 2, spheres_here * 6)
    tile = jnp.pad(tile, ((0, TILE_ROWS - tile.shape[0]), (0, TILE_LANES - tile.shape[1])))
    gathered = gather_tiles(tile).reshape(-1, TILE_LANES)
    matrix = jnp.asarray(combine_matrix(column_count, row_count, per_sphere))
    moved = jnp.dot(matrix, gathered, precision=lax.Precision.HIGHEST)
    moved = moved[:, : spheres_here * 6].reshape(-1, 6)
    all_spheres = jnp.arange(moved.shape[0], dtype=jnp.int32)
    mine = here * spheres_here + jnp.arange(spheres_here, dtype=jnp.int32)
    own = (mine[:, None] == all_spheres[None, :]).astype(jnp.float32)
    acts = (contact_sphere[None, :] == mine[:, None]).astype(jnp.float32)
    partner = (contact_partner[:, None] == all_spheres[None, :]).astype(jnp.float32)
    linked = jnp.sum(acts[:, :, None] * partner[None], axis=1)
    linked = linked - jnp.sum(acts, axis=1)[:, None] * own
    linear_part = jnp.dot(own + DASHPOT * linked, moved[:, :3], precision=lax.Precision.HIGHEST)
    angular_part = jnp.dot(own, moved[:, 3:], precision=lax.Precision.HIGHEST)
    new_motion = jnp.concatenate([linear_part, angular_part], axis=1).T
    return (state, new_motion)


def solution(mesh):
    placed = (
        P(None, "gx", "gy", None),
        P(("gx", "gy"), None),
        P(("gx", "gy")),
        P(("gx", "gy")),
        P(("gx", "gy")),
        P(None, ("gx", "gy")),
        P(None, ("gx", "gy")),
        P(None, ("gx", "gy")),
        P(("gx", "gy")),
        P(("gx", "gy")),
    )
    return jax.shard_map(
        on_device,
        mesh=mesh,
        in_specs=placed,
        out_specs=(P(None, "gx", "gy", None), P(None, ("gx", "gy"))),
        check_vma=False,
    )
```
